32 devices in a mesh: outer: 4 (over z), inner: 2 (over x), head: 4 (over y, core).
Axes of the slice: x: 2, y: 2, z: 4, core: 2. Of those that a mesh axis runs over, the one named last changes fastest.
Arguments:
- queries: bfloat16 [8192, 1024], P(('outer', 'inner'), 'head'), may hold values from -10 to 10
- keys: bfloat16 [8192, 128], P(('outer', 'inner', 'head')), may hold values from -10 to 10
- values: bfloat16 [8192, 128], P(('outer', 'inner', 'head')), may hold values from -6 to 6
- doc_lengths: int32 [4], replicated, may hold values from 1 to 3584, as said below
- block_count: int32 [8], replicated, may hold values from 1 to 2, as said below
Outputs:
- attended: bfloat16 [8192, 1024], P(('outer', 'inner'), 'head')
The draws below stay inside these ranges and needn't reach their ends.
Inputs may be any that keep to these rules, and one draw needn't show every extreme that they name: `doc_lengths`: the lengths sum to 6144, and one rollout has exactly 3584 tokens. `block_count`: exactly half of the 8 context devices hold 2 blocks and the others 1; where 8 >= 16, 8 consecutive context devices hold 1 block each; the blocks follow one another in device order.
All inputs are finite; a program needn't handle non-finite values.
Results may differ from the reference program's by a relative error of at most 0.0032.
Values may be sent and summed in bfloat16 or wider, within the bound.
No kernel may reach another device: no remote copies, remote signals or barrier semaphores. Data moves between devices by JAX's collectives and lax.ppermute only.
A program may use at most 64 MiB of HBM per device.

```python
import math
import jax
import jax.numpy as jnp
from jax import lax

HEAD_DIM = 128
GROUP_HEADS = 8
BLOCK = 512
SLOTS = 2
REACH = 7
CONTEXT = 8
NBLOCKS = 12
TOKENS = 6144
ROWS = 8192
LONGEST = 3584
DOCUMENTS = 4


def draw_queries(key, part):
    noise_key = jax.random.fold_in(key, 3)
    base = jnp.clip(1.5 * jax.random.normal(noise_key, (ROWS, GROUP_HEADS * HEAD_DIM), jnp.float32), -9.0, 9.0)
    return base.astype(jnp.bfloat16)


def draw_keys(key, part):
    noise_key = jax.random.fold_in(key, 5)
    base = jnp.clip(1.5 * jax.random.normal(noise_key, (ROWS, HEAD_DIM), jnp.float32), -9.0, 9.0)
    return base.astype(jnp.bfloat16)


def pack_layout(key):
    base_key = jax.random.fold_in(key, 31)
    run_key, shuffle_key, offset_key, jitter_key = jax.random.split(base_key, 4)
    device_index = jnp.arange(CONTEXT, dtype=jnp.int32)
    if CONTEXT >= 2 * (REACH + 1):
        run_length = REACH + 1
        run_start = jax.random.randint(run_key, (), 0, CONTEXT - run_length + 1, dtype=jnp.int32)
        shuffled = jax.random.permutation(shuffle_key, CONTEXT - run_length)
        others = (1 + (shuffled < CONTEXT // 2).astype(jnp.int32)).astype(jnp.int32)
        in_run = (device_index >= run_start) & (device_index < run_start + run_length)
        other_index = jnp.where(device_index < run_start, device_index, device_index - run_length)
        other_index = jnp.clip(other_index, 0, CONTEXT - run_length - 1)
        counts = jnp.where(in_run, 1, others[other_index]).astype(jnp.int32)
        blocks_before = jnp.sum(jnp.where(device_index < run_start, counts, 0)).astype(jnp.int32)
        first_block = jnp.minimum(blocks_before, NBLOCKS - REACH - 1)
    else:
        shuffled = jax.random.permutation(shuffle_key, CONTEXT)
        counts = (1 + (shuffled < CONTEXT // 2).astype(jnp.int32)).astype(jnp.int32)
        first_block = jnp.zeros((), jnp.int32)
    offset = jax.random.randint(offset_key, (), BLOCK // 4, BLOCK - BLOCK // 4, dtype=jnp.int32)
    return (counts, (first_block * BLOCK + offset).astype(jnp.int32), jitter_key)


def cut_points(total, count, raw, others):
    index = jnp.arange(others + 1, dtype=jnp.int32)
    safe = jnp.maximum(count, 1)
    low = total // safe
    high = (total + safe - 1) // safe
    spread = jnp.maximum(jnp.minimum(low // 4, (LONGEST - high) // 2), 0)
    jitter = raw % (2 * spread + 1) - spread
    inside = (index > 0) & (index < count)
    return index * total // safe + jnp.where(inside, jitter, 0)


def draw_doc_lengths(key, part):
    counts, before, jitter_key = pack_layout(key)
    others = DOCUMENTS - 1
    after = TOKENS - LONGEST - before
    lead = jnp.clip(before * others // (before + after), (before + LONGEST - 1) // LONGEST, others - (after + LONGEST - 1) // LONGEST).astype(jnp.int32)
    trail = (others - lead).astype(jnp.int32)
    lead_key, trail_key = jax.random.split(jitter_key, 2)
    lead_raw = jax.random.randint(lead_key, (others + 1,), 0, 1 << 20, dtype=jnp.int32)
    trail_raw = jax.random.randint(trail_key, (others + 1,), 0, 1 << 20, dtype=jnp.int32)
    lead_cuts = cut_points(before, lead, lead_raw, others)
    trail_cuts = cut_points(after, trail, trail_raw, others)
    lead_sizes = lead_cuts[1:] - lead_cuts[:-1]
    trail_sizes = trail_cuts[1:] - trail_cuts[:-1]
    slot = jnp.arange(DOCUMENTS, dtype=jnp.int32)
    lead_pick = lead_sizes[jnp.clip(slot, 0, others - 1)]
    trail_pick = trail_sizes[jnp.clip(slot - lead - 1, 0, others - 1)]
    lengths = jnp.where(slot < lead, lead_pick, jnp.where(slot == lead, LONGEST, trail_pick))
    return lengths.astype(jnp.int32)


def draw_block_count(key, part):
    counts, before, jitter_key = pack_layout(key)
    return counts


def levels(key, shape, shards, least, largest):
    def one(dim, blocks):
        draws = jax.random.uniform(jax.random.fold_in(jax.random.fold_in(key, 6), dim), (blocks,), jnp.float32, least / len(shards), largest / len(shards))
        return jnp.repeat(jnp.exp(draws), shape[dim] // blocks).reshape((-1,) + (1,) * (len(shape) - dim - 1))

    loudness = one(*shards[0])
    for cut in shards[1:]:
        loudness = loudness * one(*cut)
    return loudness


def scatter_about(key, shape, deviation, limit, cuts=(), kind=jnp.bfloat16):
    level = levels(key, shape, cuts, -0.22, 0.18) if cuts else 1.0
    values = jax.random.normal(key, shape, jnp.float32) * deviation * level
    return jnp.minimum(jnp.maximum(values, -limit), limit).astype(kind)


def setup_inputs(seed: int = 0) -> dict:
    arg_keys = jax.random.split(jax.random.key(seed), 6)
    queries = draw_queries(jax.random.fold_in(arg_keys[5], 71), 0)
    keys = draw_keys(jax.random.fold_in(arg_keys[5], 71), 0)
    values = scatter_about(arg_keys[2], (ROWS, HEAD_DIM), 1.0, 6.0, ((0, 32),))
    doc_lengths = draw_doc_lengths(jax.random.fold_in(arg_keys[5], 71), 0)
    block_count = draw_block_count(jax.random.fold_in(arg_keys[5], 71), 0)
    return dict(queries=queries, keys=keys, values=values, doc_lengths=doc_lengths, block_count=block_count)


NEGATIVE = -1e+30

def reference(queries, keys, values, doc_lengths, block_count):
    block_rows = SLOTS * BLOCK
    context = block_count.shape[0]
    starts = ((jnp.cumsum(block_count) - block_count) * BLOCK).astype(jnp.int32)
    offsets = jnp.arange(block_rows, dtype=jnp.int32)
    position = (starts[:, None] + offsets[None, :]).astype(jnp.int32)
    is_live = offsets[None, :] < (block_count * BLOCK)[:, None]
    bounds = jnp.cumsum(doc_lengths).astype(jnp.int32)
    doc_ids = lax.optimization_barrier(jnp.sum((position[:, :, None] >= bounds[None, None, :]).astype(jnp.int32), axis=2)).astype(jnp.int32)

    def padded(array, fill):
        front = jnp.full((REACH,) + array.shape[1:], fill, array.dtype)
        return jnp.concatenate([front, array], axis=0)
    key_units = padded(keys.reshape(context, block_rows, HEAD_DIM), 0)
    value_units = padded(values.reshape(context, block_rows, HEAD_DIM), 0)
    pos_units = padded(position, 0)
    live_units = padded(is_live, False)
    doc_units = padded(doc_ids, -1)
    query_units = queries.reshape(context, block_rows, GROUP_HEADS, HEAD_DIM)
    score_scale = 1.0 / math.sqrt(HEAD_DIM)

    def one_device(index):

        def window_of(array):
            taken = lax.dynamic_slice_in_dim(array, index, REACH + 1, 0)
            return taken.reshape((-1,) + array.shape[2:])
        key_rows = window_of(key_units).astype(jnp.float32)
        value_rows = window_of(value_units).astype(jnp.float32)
        key_pos = window_of(pos_units)
        key_live = window_of(live_units)
        key_doc = window_of(doc_units)
        query_rows = lax.dynamic_index_in_dim(query_units, index, 0, keepdims=False).astype(jnp.float32)
        own_pos = lax.dynamic_index_in_dim(position, index, 0, keepdims=False)
        own_live = lax.dynamic_index_in_dim(is_live, index, 0, keepdims=False)
        own_doc = lax.dynamic_index_in_dim(doc_ids, index, 0, keepdims=False)
        visible = own_live[:, None] & key_live[None, :] & (own_doc[:, None] == key_doc[None, :]) & (key_pos[None, :] <= own_pos[:, None])
        scores = jnp.einsum('qhd,kd->qhk', query_rows, key_rows) * score_scale
        masked = jnp.where(visible[:, None, :], scores, NEGATIVE)
        row_top = lax.optimization_barrier(jnp.max(masked, axis=2))
        weights = jnp.where(visible[:, None, :], jnp.exp(masked - row_top[:, :, None]), 0.0)
        row_total = lax.optimization_barrier(jnp.sum(weights, axis=2))
        rounded = lax.optimization_barrier(weights.astype(jnp.bfloat16)).astype(jnp.float32)
        weighted = jnp.einsum('qhk,kd->qhd', rounded, value_rows)
        result = jnp.where(own_live[:, None, None], weighted / jnp.where(own_live[:, None], row_total, 1.0)[:, :, None], 0.0)
        return result.astype(jnp.bfloat16)
    outputs = lax.map(one_device, jnp.arange(context, dtype=jnp.int32))
    return outputs.reshape(context * block_rows, GROUP_HEADS * HEAD_DIM)
```

```python
import functools
import math

import jax
import jax.numpy as jnp
from jax import lax
from jax.experimental import pallas as pl
from jax.experimental.pallas import tpu as pltpu
from jax.sharding import PartitionSpec as P

BLOCK = 512
REACH = 7
PAIR = 2
NEGATIVE = -1e30
AXES = ("outer", "inner", "head")


def attend_kernel(cfg, place, lengths, counts, q_ref, *refs):
    delta, tiles, heads, tile_q, first, last = cfg
    piece_refs = refs[: 2 * tiles]
    refs = refs[2 * tiles :]
    if first:
        top_in = acc_in = None
    else:
        top_in, acc_in = refs[:2]
        refs = refs[2:]
    if last:
        out_ref = refs[0]
        refs = refs[1:]
        k_all, v_all, first_key, top, acc, starts = refs
    else:
        top, acc = refs[:2]
        k_all, v_all, first_key, starts = refs[2:]
    rows = q_ref.shape[0]
    dim = k_all.shape[2]
    tile_k = k_all.shape[1]
    piece = tile_k // PAIR
    spread = tiles // PAIR
    context = counts.shape[0]
    documents = lengths.shape[0]
    device = place[0]
    head_index = place[1]
    core = lax.rem(head_index, PAIR)
    side = head_index // PAIR
    scale = math.log2(math.e) / math.sqrt(dim)

    for tile in range(tiles):
        for step in range(PAIR):
            source = piece_refs[tile * PAIR + step]
            slot = core if step == 0 else 1 - core
            at = pl.ds(pl.multiple_of(slot * piece, piece), piece)
            k_all[tile, at, :] = source[:piece, :]
            v_all[tile, at, :dim] = source[piece:, :]
        v_all[tile, :, dim:] = jnp.ones((tile_k, dim), jnp.bfloat16)

    def fill(index, total):
        starts[index] = total
        return total + counts[index] * BLOCK

    lax.fori_loop(0, context, fill, jnp.int32(0))
    own_start = starts[device]
    own_live = counts[device] * BLOCK

    def opening(position):
        def look(index, carry):
            edge, begin = carry
            edge = edge + lengths[index]
            return edge, jnp.where(edge <= position, edge, begin)

        return lax.fori_loop(0, documents, look, (jnp.int32(0), jnp.int32(0)))[1]

    if first:
        top[...] = jnp.full(top.shape, NEGATIVE, jnp.float32)
        acc[...] = jnp.zeros(acc.shape, jnp.float32)
    else:
        top[...] = top_in[...]
        acc[...] = acc_in[...]

    def wide(value, times):
        return jnp.concatenate([value] * times, axis=1)

    def attend(tile_index, at, key_start, query_start, masked):
        if masked:
            key_position = key_start + lax.broadcasted_iota(jnp.int32, (tile_q, tile_k), 1)
            query_position = query_start + lax.broadcasted_iota(jnp.int32, (tile_q, tile_k), 0)
            visible = (key_position <= query_position) & (
                key_position >= wide(first_key[at, :], tile_k // dim)
            )
        for head in range(heads):
            scores = lax.dot_general(
                q_ref[at, head * dim : (head + 1) * dim],
                k_all[tile_index],
                (((1,), (1,)), ((), ())),
                preferred_element_type=jnp.float32,
            )
            if masked:
                scores = jnp.where(visible, scores, NEGATIVE)
            before = top[head, at, :]
            after = jnp.maximum(before, jnp.max(scores, axis=1, keepdims=True))
            factor = jnp.exp2((before - after) * scale)
            weights = jnp.exp2((scores - wide(after, tile_k // dim)) * scale)
            added = jnp.dot(
                weights.astype(jnp.bfloat16), v_all[tile_index], preferred_element_type=jnp.float32
            )
            acc[head, at, :] = acc[head, at, :] * wide(factor, 2) + added
            top[head, at, :] = after

    def query_tile(index, unused):
        row = index * tile_q
        at = pl.ds(pl.multiple_of(row, tile_q), tile_q)
        query_start = own_start + row
        query_end = query_start + tile_q - 1

        @pl.when(row < own_live)
        def _():
            opened_low = opening(query_start)
            opened_high = opening(query_end)
            position = query_start + lax.broadcasted_iota(jnp.int32, (tile_q, dim), 0)

            def look(index, carry):
                edge, begin = carry
                edge = edge + lengths[index]
                return edge, jnp.where(position >= edge, edge, begin)

            first_key[at, :] = lax.fori_loop(
                0, documents, look, (jnp.int32(0), jnp.zeros((tile_q, dim), jnp.int32))
            )[1]

            def key_tile(tile_index, unused):
                across = tile_index // spread
                along = lax.rem(tile_index, spread)
                level = device // PAIR - delta
                member = lax.rem(device, PAIR)
                member = jnp.where(across == 1, 1 - member, member)
                source = level * PAIR + member
                clipped = jnp.maximum(source, 0)
                offset = lax.rem(side + spread - along, spread) * tile_k
                key_start = starts[clipped] + offset
                key_end = key_start + tile_k - 1
                active = (
                    (level >= 0)
                    & (offset < counts[clipped] * BLOCK)
                    & (key_start <= query_end)
                    & (key_end >= opened_low)
                )
                whole = (key_end <= query_start) & (key_start >= opened_high)

                @pl.when(active & whole)
                def _():
                    attend(tile_index, at, key_start, query_start, False)

                @pl.when(active & jnp.logical_not(whole))
                def _():
                    attend(tile_index, at, key_start, query_start, True)

                return 0

            lax.fori_loop(0, tiles, key_tile, 0)

        if last:

            @pl.when(row < own_live)
            def _():
                for head in range(heads):
                    total = acc[head, at, dim:]
                    out_ref[at, head * dim : (head + 1) * dim] = (
                        acc[head, at, :dim] / total
                    ).astype(jnp.bfloat16)

            @pl.when(row >= own_live)
            def _():
                out_ref[at, :] = jnp.zeros((tile_q, heads * dim), jnp.bfloat16)

        return 0

    lax.fori_loop(0, rows // tile_q, query_tile, 0)


def attend(delta, place, lengths, counts, queries, pieces, state, last):
    rows, width = queries.shape
    piece_rows, dim = pieces[0].shape
    heads = width // dim
    tile_k = piece_rows // 2 * PAIR
    tiles = len(pieces) // PAIR
    tile_q = min(rows, 512)
    first = state is None
    scalar = pl.BlockSpec(memory_space=pltpu.SMEM)
    vector = pl.BlockSpec(memory_space=pltpu.VMEM)
    top = (heads, rows, dim)
    acc = (heads, rows, 2 * dim)
    scratch = [
        pltpu.VMEM((tiles, tile_k, dim), jnp.bfloat16),
        pltpu.VMEM((tiles, tile_k, 2 * dim), jnp.bfloat16),
        pltpu.VMEM((rows, dim), jnp.int32),
    ]
    if last:
        out_shape = jax.ShapeDtypeStruct((rows, width), jnp.bfloat16)
        scratch += [pltpu.VMEM(top, jnp.float32), pltpu.VMEM(acc, jnp.float32)]
    else:
        out_shape = (
            jax.ShapeDtypeStruct(top, jnp.float32),
            jax.ShapeDtypeStruct(acc, jnp.float32),
        )
    scratch += [pltpu.SMEM((counts.shape[0],), jnp.int32)]
    carried = () if first else state
    pairs = (rows // tile_q) * tiles * heads
    return pl.pallas_call(
        functools.partial(attend_kernel, (delta, tiles, heads, tile_q, first, last)),
        out_shape=out_shape,
        in_specs=[scalar] * 3 + [vector] * (1 + len(pieces) + len(carried)),
        out_specs=vector if last else (vector, vector),
        scratch_shapes=scratch,
        compiler_params=pltpu.CompilerParams(vmem_limit_bytes=32 << 20),
        cost_estimate=pl.CostEstimate(
            flops=pairs * tile_q * tile_k * dim * 4,
            bytes_accessed=pairs * tile_q * dim * 4,
            transcendentals=pairs * tile_q * tile_k,
        ),
        name=f"attend_{delta}",
    )(place, lengths, counts, queries, *pieces, *carried)


def solution(mesh):
    contexts = mesh.shape["outer"] * mesh.shape["inner"]
    group = mesh.shape["head"]
    levels = contexts // PAIR
    sides = group // PAIR
    farthest = min((REACH + PAIR - 1) // PAIR, levels - 1)

    def moved(value, target):
        pairs = []
        for level in range(levels):
            for member in range(PAIR):
                for side in range(sides):
                    for core in range(PAIR):
                        place = (level, member, side, core)
                        to = target(*place)
                        pairs.append(tuple(
                            ((a * PAIR + b) * sides + c) * PAIR + d for a, b, c, d in (place, to)
                        ))
        return lax.ppermute(value, AXES, pairs)

    def ahead(value, delta):
        return moved(value, lambda l, m, s, c: ((l + delta) % levels, m, s, c))

    def spread(value):
        found = []
        for across in range(PAIR):
            for along in range(sides):
                held = value
                if across or along:
                    held = moved(
                        value, lambda l, m, s, c: (l, (m + across) % PAIR, (s + along) % sides, c)
                    )
                found += [held, moved(held, lambda l, m, s, c: (l, m, s, 1 - c))]
        return found

    def needed(delta, lengths, counts):
        ends = jnp.cumsum(counts) * BLOCK
        begins = ends - counts * BLOCK
        edges = jnp.cumsum(lengths)
        opened = jnp.max(
            jnp.where(edges[None, :] <= begins[:, None], edges[None, :], 0), axis=1
        )
        before = ends.reshape(levels, PAIR)[:-delta, PAIR - 1]
        return jnp.any(jnp.min(opened.reshape(levels, PAIR)[delta:], axis=1) < before)

    def shards(queries, keys, values, lengths, counts):
        device = lax.axis_index(("outer", "inner"))
        place = jnp.stack([device, lax.axis_index("head")]).astype(jnp.int32)
        step = functools.partial(attend, place=place, lengths=lengths, counts=counts, queries=queries)
        own = jnp.concatenate([keys, values], axis=0)
        near = [own] + [ahead(own, delta) for delta in range(1, min(farthest, 2) + 1)]
        state = None
        for delta in range(len(near) - 1):
            state = step(delta, pieces=spread(near[delta]), state=state, last=False)
        delta = len(near) - 1
        pieces = spread(near[delta])
        if farthest == delta:
            return step(delta, pieces=pieces, state=state, last=True)

        def short(operands):
            near, pieces, state = operands
            return step(delta, pieces=pieces, state=state, last=True)

        def long(operands):
            near, pieces, state = operands
            state = step(delta, pieces=pieces, state=state, last=False)
            for further in range(delta + 1, farthest + 1):
                near = ahead(near, 1)
                state = step(
                    further, pieces=spread(near), state=state, last=further == farthest
                )
            return state

        return lax.cond(
            needed(delta + 1, lengths, counts), long, short, (near[delta], pieces, state)
        )

    placed = (
        P(("outer", "inner"), "head"),
        P(AXES, None),
        P(AXES, None),
        P(),
        P(),
    )
    return jax.shard_map(
        shards, mesh=mesh, in_specs=placed, out_specs=P(("outer", "inner"), "head"), check_vma=False
    )
```

```python
import functools
import math

import jax
import jax.numpy as jnp
from jax import lax
from jax.experimental import pallas as pl
from jax.experimental.pallas import tpu as pltpu
from jax.sharding import PartitionSpec as P

BLOCK = 512
REACH = 7
PAIR = 2
FIELDS = 6
NEGATIVE = -1e30
AXES = ("outer", "inner", "head")


def join_kernel(keys, values, joined, semaphores):
    rows = keys.shape[0]
    copies = [
        pltpu.make_async_copy(keys, joined.at[:rows], semaphores.at[0]),
        pltpu.make_async_copy(values, joined.at[rows:], semaphores.at[1]),
    ]
    for copy in copies:
        copy.start()
    for copy in copies:
        copy.wait()


def join(keys, values):
    rows, dim = keys.shape
    return pl.pallas_call(
        join_kernel,
        out_shape=jax.ShapeDtypeStruct((2 * rows, dim), keys.dtype),
        in_specs=[pl.BlockSpec(memory_space=pl.ANY)] * 2,
        out_specs=pl.BlockSpec(memory_space=pltpu.VMEM),
        scratch_shapes=[pltpu.SemaphoreType.DMA((2,))],
        compiler_params=pltpu.CompilerParams(vmem_limit_bytes=4 << 20),
        name="join",
    )(keys, values)


def attend_kernel(cfg, place, lengths, counts, q_ref, *refs):
    delta, tiles, heads, tile_q, first, last, further = cfg
    piece_refs = refs[: PAIR * tiles]
    refs = refs[PAIR * tiles :]
    if last:
        top_all, acc_all, out_ref = refs[:3]
        refs = refs[3:]
    elif first:
        top_all, acc_all, flag = refs[:3]
        refs = refs[3:]
    else:
        top_all, acc_all = refs[2:4]
        refs = refs[4:]
    k_all, v_all, score_a, score_b, top, acc, starts, work = refs
    rows = q_ref.shape[0]
    dim = k_all.shape[2]
    tile_k = k_all.shape[1]
    piece = tile_k // PAIR
    spread = tiles // PAIR
    context = counts.shape[0]
    documents = lengths.shape[0]
    device = place[0]
    head_index = place[1]
    core = lax.rem(head_index, PAIR)
    side = head_index // PAIR
    scale = math.log2(math.e) / math.sqrt(dim)

    def fill(index, total):
        starts[index] = total
        return total + counts[index] * BLOCK

    starts[context] = lax.fori_loop(0, context, fill, jnp.int32(0))
    own_start = starts[device]
    own_live = counts[device] * BLOCK

    def opening(position):
        def look(index, carry):
            edge, begin = carry
            edge = edge + lengths[index]
            return edge, jnp.where(edge <= position, edge, begin)

        return lax.fori_loop(0, documents, look, (jnp.int32(0), jnp.int32(0)))[1]

    if first:
        def reaches(level, found):
            before = starts[(level - further + 1) * PAIR]
            return found | (opening(starts[level * PAIR]) < before).astype(jnp.int32)

        flag[0] = lax.fori_loop(further, context // PAIR, reaches, jnp.int32(0))

    for tile in range(tiles):
        for step in range(PAIR):
            source = piece_refs[tile * PAIR + step]
            slot = core if step == 0 else 1 - core
            at = pl.ds(pl.multiple_of(slot * piece, piece), piece)
            k_all[tile, at, :] = source[:piece, :]
            v_all[tile, at, :dim] = source[piece:, :]
        v_all[tile, :, dim:] = jnp.ones((tile_k, dim), jnp.bfloat16)

    def finish(index, acc_ref):
        at = pl.ds(pl.multiple_of(index * tile_q, tile_q), tile_q)
        for head in range(heads):
            out_ref[at, head * dim : (head + 1) * dim] = (
                acc_ref[head, :, :dim] / acc_ref[head, :, dim:]
            ).astype(jnp.bfloat16)

    def plan_queries(index, count):
        row = index * tile_q
        query_start = own_start + row
        query_end = query_start + tile_q - 1
        opened_low = opening(query_start)
        opened_high = opening(query_end)

        def plan_keys(tile, carry):
            count, opener = carry
            level = device // PAIR - delta
            member = lax.rem(device, PAIR)
            member = jnp.where(tile // spread == 1, 1 - member, member)
            source = jnp.maximum(level * PAIR + member, 0)
            offset = lax.rem(side + spread - lax.rem(tile, spread), spread) * tile_k
            key_start = starts[source] + offset
            key_end = key_start + tile_k - 1
            active = (
                (level >= 0)
                & (row < own_live)
                & (offset < counts[source] * BLOCK)
                & (key_start <= query_end)
                & (key_end >= opened_low)
            )
            whole = (key_end <= query_start) & (key_start >= opened_high)
            at = count * FIELDS
            work[at] = index
            work[at + 1] = tile
            work[at + 2] = whole.astype(jnp.int32)
            work[at + 3] = key_start
            work[at + 4] = opener
            work[at + 5] = 0
            return jnp.where(active, count + 1, count), jnp.where(active, 0, opener)

        after = lax.fori_loop(0, tiles, plan_keys, (count, jnp.int32(1)))[0]

        @pl.when(after > count)
        def _():
            work[(after - 1) * FIELDS + 5] = 1

        if last:

            @pl.when((after == count) & (row < own_live))
            def _():
                finish(index, acc_all.at[index])

            @pl.when(row >= own_live)
            def _():
                at = pl.ds(pl.multiple_of(row, tile_q), tile_q)
                out_ref[at, :] = jnp.zeros((tile_q, heads * dim), jnp.bfloat16)

        return after

    total = lax.fori_loop(0, rows // tile_q, plan_queries, jnp.int32(0))
    work[total * FIELDS] = 0
    work[total * FIELDS + 1] = 0

    def wide(value, times):
        return jnp.concatenate([value] * times, axis=1)

    def score(item, head):
        at = pl.ds(pl.multiple_of(work[item * FIELDS] * tile_q, tile_q), tile_q)
        return lax.dot_general(
            q_ref[at, head * dim : (head + 1) * dim],
            k_all[work[item * FIELDS + 1]],
            (((1,), (1,)), ((), ())),
            preferred_element_type=jnp.float32,
        )

    def handle(item, current, coming):
        base = item * FIELDS
        query_index = work[base]
        whole = work[base + 2]

        @pl.when(work[base + 4] == 1)
        def _():
            if first:
                top[...] = jnp.full(top.shape, NEGATIVE, jnp.float32)
                acc[...] = jnp.zeros(acc.shape, jnp.float32)
            else:
                top[...] = top_all[query_index]
                acc[...] = acc_all[query_index]

        def run(masked):
            v_tile = v_all[work[base + 1]]
            if masked:
                row = own_start + query_index * tile_q
                narrow = row + lax.broadcasted_iota(jnp.int32, (tile_q, dim), 0)

                def look(index, carry):
                    edge, begin = carry
                    edge = edge + lengths[index]
                    return edge, jnp.where(narrow >= edge, edge, begin)

                opened = lax.fori_loop(
                    0, documents, look, (jnp.int32(0), jnp.zeros((tile_q, dim), jnp.int32))
                )[1]
                key_position = work[base + 3] + lax.broadcasted_iota(
                    jnp.int32, (tile_q, tile_k), 1
                )
                visible = (key_position <= wide(narrow, tile_k // dim)) & (
                    key_position >= wide(opened, tile_k // dim)
                )
            for head in range(heads):
                coming[head] = score(item + 1, head)
                scores = current[head]
                if masked:
                    scores = jnp.where(visible, scores, NEGATIVE)
                before = top[head]
                after = jnp.maximum(before, jnp.max(scores, axis=1, keepdims=True))
                weights = jnp.exp2((scores - wide(after, tile_k // dim)) * scale)
                factor = jnp.exp2((before - after) * scale)
                top[head] = after
                acc[head] = acc[head] * wide(factor, 2) + jnp.dot(
                    weights.astype(jnp.bfloat16), v_tile, preferred_element_type=jnp.float32
                )

        @pl.when(whole == 1)
        def _():
            run(False)

        @pl.when(whole == 0)
        def _():
            run(True)

        @pl.when(work[base + 5] == 1)
        def _():
            if last:
                finish(query_index, acc)
            else:
                top_all[query_index] = top[...]
                acc_all[query_index] = acc[...]

    @pl.when(total > 0)
    def _():
        for head in range(heads):
            score_a[head] = score(0, head)

    def two(index, unused):
        handle(2 * index, score_a, score_b)

        @pl.when(2 * index + 1 < total)
        def _():
            handle(2 * index + 1, score_b, score_a)

        return 0

    lax.fori_loop(0, (total + 1) // 2, two, 0)


def attend(delta, place, lengths, counts, queries, pieces, state, last, further=0):
    rows, width = queries.shape
    piece_rows, dim = pieces[0].shape
    heads = width // dim
    tile_k = piece_rows // 2 * PAIR
    tiles = len(pieces) // PAIR
    tile_q = min(rows, BLOCK)
    steps = rows // tile_q
    first = state is None
    scalar = pl.BlockSpec(memory_space=pltpu.SMEM)
    vector = pl.BlockSpec(memory_space=pltpu.VMEM)
    top = (heads, tile_q, dim)
    acc = (heads, tile_q, 2 * dim)
    scratch = [
        pltpu.VMEM((tiles, tile_k, dim), jnp.bfloat16),
        pltpu.VMEM((tiles, tile_k, 2 * dim), jnp.bfloat16),
        pltpu.VMEM((heads, tile_q, tile_k), jnp.float32),
        pltpu.VMEM((heads, tile_q, tile_k), jnp.float32),
        pltpu.VMEM(top, jnp.float32),
        pltpu.VMEM(acc, jnp.float32),
        pltpu.SMEM((counts.shape[0] + 1,), jnp.int32),
        pltpu.SMEM((FIELDS * (steps * tiles + 2),), jnp.int32),
    ]
    aliases = {}
    if last:
        out_shape = jax.ShapeDtypeStruct((rows, width), jnp.bfloat16)
        out_specs = vector
    else:
        out_shape = (
            jax.ShapeDtypeStruct((steps,) + top, jnp.float32),
            jax.ShapeDtypeStruct((steps,) + acc, jnp.float32),
        )
        out_specs = (vector, vector)
        if first:
            out_shape += (jax.ShapeDtypeStruct((1,), jnp.int32),)
            out_specs += (scalar,)
        else:
            aliases = {4 + len(pieces): 0, 5 + len(pieces): 1}
    carried = () if first else state
    pairs = steps * tiles * heads
    return pl.pallas_call(
        functools.partial(attend_kernel, (delta, tiles, heads, tile_q, first, last, further)),
        out_shape=out_shape,
        in_specs=[scalar] * 3 + [vector] * (1 + len(pieces) + len(carried)),
        out_specs=out_specs,
        scratch_shapes=scratch,
        input_output_aliases=aliases,
        compiler_params=pltpu.CompilerParams(vmem_limit_bytes=24 << 20),
        cost_estimate=pl.CostEstimate(
            flops=pairs * tile_q * tile_k * dim * 4,
            bytes_accessed=pairs * tile_q * dim * 4,
            transcendentals=pairs * tile_q * tile_k,
        ),
    )(place, lengths, counts, queries, *pieces, *carried)


def solution(mesh):
    contexts = mesh.shape["outer"] * mesh.shape["inner"]
    group = mesh.shape["head"]
    levels = contexts // PAIR
    sides = group // PAIR
    farthest = min((REACH + PAIR - 1) // PAIR, levels - 1)
    near_count = min(farthest, 2)

    def moved(value, target):
        pairs = []
        for level in range(levels):
            for member in range(PAIR):
                for side in range(sides):
                    for core in range(PAIR):
                        place = (level, member, side, core)
                        to = target(*place)
                        pairs.append(tuple(
                            ((a * PAIR + b) * sides + c) * PAIR + d for a, b, c, d in (place, to)
                        ))
        return lax.ppermute(value, AXES, pairs)

    def ahead(value, delta):
        return moved(value, lambda l, m, s, c: ((l + delta) % levels, m, s, c))

    def spread(value):
        found = []
        for across in range(PAIR):
            for along in range(sides):
                held = value
                if across or along:
                    held = moved(
                        value, lambda l, m, s, c: (l, (m + across) % PAIR, (s + along) % sides, c)
                    )
                found += [held, moved(held, lambda l, m, s, c: (l, m, s, 1 - c))]
        return found

    def layer(queries, keys, values, lengths, counts):
        device = lax.axis_index(("outer", "inner"))
        place = jnp.stack([device, lax.axis_index("head")]).astype(jnp.int32)

        def step(delta, **rest):
            return attend(
                delta, place=place, lengths=lengths, counts=counts, queries=queries, **rest
            )

        own = join(keys, values)
        near = [own] + [ahead(own, delta) for delta in range(1, near_count + 1)]
        state = None
        reach = None
        for delta in range(near_count):
            state = step(
                delta,
                pieces=spread(near[delta]),
                state=state,
                last=False,
                further=near_count + 1,
            )
            if delta == 0:
                reach = state[2]
                state = state[:2]
        delta = near_count
        pieces = spread(near[delta])
        if farthest == delta:
            return step(delta, pieces=pieces, state=state, last=True)

        def short(operands):
            _, pieces, state = operands
            return step(delta, pieces=pieces, state=state, last=True)

        def long(operands):
            near, pieces, state = operands
            state = step(delta, pieces=pieces, state=state, last=False)
            for further in range(delta + 1, farthest + 1):
                near = ahead(near, 1)
                state = step(further, pieces=spread(near), state=state, last=further == farthest)
            return state

        return lax.cond(reach[0] != 0, long, short, (near[delta], pieces, state))

    placed = (
        P(("outer", "inner"), "head"),
        P(AXES, None),
        P(AXES, None),
        P(),
        P(),
    )
    return jax.shard_map(
        layer, mesh=mesh, in_specs=placed, out_specs=P(("outer", "inner"), "head"), check_vma=False
    )
```

```python
import functools
import math

import jax
import jax.numpy as jnp
from jax import lax
from jax.experimental import pallas as pl
from jax.experimental.pallas import tpu as pltpu
from jax.sharding import PartitionSpec as P

BLOCK = 512
REACH = 7
PAIR = 2
FIELDS = 6
NEGATIVE = -1e30
AXES = ("outer", "inner", "head")


def join_kernel(keys, values, joined, semaphores):
    rows = keys.shape[0]
    copies = [
        pltpu.make_async_copy(keys, joined.at[:rows], semaphores.at[0]),
        pltpu.make_async_copy(values, joined.at[rows:], semaphores.at[1]),
    ]
    for copy in copies:
        copy.start()
    for copy in copies:
        copy.wait()


def join(keys, values):
    rows, dim = keys.shape
    return pl.pallas_call(
        join_kernel,
        out_shape=jax.ShapeDtypeStruct((2 * rows, dim), keys.dtype),
        in_specs=[pl.BlockSpec(memory_space=pltpu.MemorySpace.HBM)] * 2,
        out_specs=pl.BlockSpec(memory_space=pltpu.VMEM),
        scratch_shapes=[pltpu.SemaphoreType.DMA((2,))],
        compiler_params=pltpu.CompilerParams(vmem_limit_bytes=4 << 20),
        name="join",
    )(keys, values)


def attend_kernel(cfg, place, lengths, counts, q_ref, *refs):
    delta, tiles, heads, tile_q, first, last, further = cfg
    piece_refs = refs[: PAIR * tiles]
    refs = refs[PAIR * tiles :]
    if last:
        top_all, acc_all, out_ref = refs[:3]
        refs = refs[3:]
    elif first:
        top_all, acc_all, flag = refs[:3]
        refs = refs[3:]
    else:
        top_all, acc_all = refs[2:4]
        refs = refs[4:]
    k_all, v_all, score_a, score_b, top, acc, opened, starts, work = refs
    rows = q_ref.shape[0]
    dim = k_all.shape[2]
    tile_k = k_all.shape[1]
    piece = tile_k // PAIR
    spread = tiles // PAIR
    context = counts.shape[0]
    documents = lengths.shape[0]
    device = place[0]
    head_index = place[1]
    core = lax.rem(head_index, PAIR)
    side = head_index // PAIR
    scale = math.log2(math.e) / math.sqrt(dim)

    def fill(index, total):
        starts[index] = total
        return total + counts[index] * BLOCK

    starts[context] = lax.fori_loop(0, context, fill, jnp.int32(0))
    own_start = starts[device]
    own_live = counts[device] * BLOCK

    def opening(position):
        def look(index, carry):
            edge, begin = carry
            edge = edge + lengths[index]
            return edge, jnp.where(edge <= position, edge, begin)

        return lax.fori_loop(0, documents, look, (jnp.int32(0), jnp.int32(0)))[1]

    if first:
        def reaches(level, found):
            before = starts[(level - further + 1) * PAIR]
            return found | (opening(starts[level * PAIR]) < before).astype(jnp.int32)

        flag[0] = lax.fori_loop(further, context // PAIR, reaches, jnp.int32(0))

    for tile in range(tiles):
        for step in range(PAIR):
            source = piece_refs[tile * PAIR + step]
            slot = core if step == 0 else 1 - core
            at = pl.ds(pl.multiple_of(slot * piece, piece), piece)
            k_all[tile, at, :] = source[:piece, :]
            v_all[tile, at, :dim] = source[piece:, :]
        v_all[tile, :, dim:] = jnp.ones((tile_k, dim), jnp.bfloat16)

    def finish(index, acc_ref):
        at = pl.ds(pl.multiple_of(index * tile_q, tile_q), tile_q)
        for head in range(heads):
            out_ref[at, head * dim : (head + 1) * dim] = (
                acc_ref[head, :, :dim] / acc_ref[head, :, dim:]
            ).astype(jnp.bfloat16)

    def plan_queries(index, count):
        row = index * tile_q
        query_start = own_start + row
        query_end = query_start + tile_q - 1
        opened_low = opening(query_start)

        def plan_keys(tile, carry):
            count, opener = carry
            level = device // PAIR - delta
            member = lax.rem(device, PAIR)
            member = jnp.where(tile // spread == 1, 1 - member, member)
            source = jnp.maximum(level * PAIR + member, 0)
            offset = lax.rem(side + spread - lax.rem(tile, spread), spread) * tile_k
            key_start = starts[source] + offset
            key_end = key_start + tile_k - 1
            active = (
                (level >= 0)
                & (row < own_live)
                & (offset < counts[source] * BLOCK)
                & (key_start <= query_end)
                & (key_end >= opened_low)
            )
            whole = (key_end <= query_start) & (key_start >= opening(key_end))
            at = count * FIELDS
            work[at] = index
            work[at + 1] = tile
            work[at + 2] = whole.astype(jnp.int32)
            work[at + 3] = key_start
            work[at + 4] = opener
            work[at + 5] = 0
            return jnp.where(active, count + 1, count), jnp.where(active, 0, opener)

        after = lax.fori_loop(0, tiles, plan_keys, (count, jnp.int32(1)))[0]

        @pl.when(after > count)
        def _():
            work[(after - 1) * FIELDS + 5] = 1

        if last:

            @pl.when((after == count) & (row < own_live))
            def _():
                finish(index, acc_all.at[index])

            @pl.when(row >= own_live)
            def _():
                at = pl.ds(pl.multiple_of(row, tile_q), tile_q)
                out_ref[at, :] = jnp.zeros((tile_q, heads * dim), jnp.bfloat16)

        return after

    total = lax.fori_loop(0, rows // tile_q, plan_queries, jnp.int32(0))
    work[total * FIELDS] = 0
    work[total * FIELDS + 1] = 0

    def wide(value, times):
        return jnp.concatenate([value] * times, axis=1)

    def score(item, head):
        at = pl.ds(pl.multiple_of(work[item * FIELDS] * tile_q, tile_q), tile_q)
        return lax.dot_general(
            q_ref[at, head * dim : (head + 1) * dim],
            k_all[work[item * FIELDS + 1]],
            (((1,), (1,)), ((), ())),
            preferred_element_type=jnp.float32,
        )

    def handle(item, current, coming):
        base = item * FIELDS
        query_index = work[base]
        whole = work[base + 2]

        @pl.when(work[base + 4] == 1)
        def _():
            row = own_start + query_index * tile_q
            position = row + lax.broadcasted_iota(jnp.int32, (tile_q, dim), 0)

            def look(index, edge):
                edge = edge + lengths[index]
                opened[...] = jnp.where(position >= edge, edge, opened[...])
                return edge

            opened[...] = jnp.zeros((tile_q, dim), jnp.int32)
            lax.fori_loop(0, documents, look, jnp.int32(0))
            if first:
                top[...] = jnp.full(top.shape, NEGATIVE, jnp.float32)
                acc[...] = jnp.zeros(acc.shape, jnp.float32)
            else:
                top[...] = top_all[query_index]
                acc[...] = acc_all[query_index]

        def run(masked):
            v_tile = v_all[work[base + 1]]
            key_start = work[base + 3]
            begin = opened[...]
            if masked:
                row = own_start + query_index * tile_q
                position = row + lax.broadcasted_iota(jnp.int32, (tile_q, dim), 0)
                behind = wide((position - begin).astype(jnp.uint32), tile_k // dim)
                key_position = key_start + lax.broadcasted_iota(jnp.int32, (1, tile_k), 1)
            else:
                seen = begin <= key_start
            for head in range(heads):
                coming[head] = score(item + 1, head)
                scores = current[head]
                before = top[head]
                if masked:
                    into = (key_position - wide(begin, tile_k // dim)).astype(jnp.uint32)
                    scores = jnp.where(into <= behind, scores, NEGATIVE)
                    after = jnp.maximum(before, jnp.max(scores, axis=1, keepdims=True))
                    taken = after
                else:
                    after = jnp.maximum(before, jnp.max(scores, axis=1, keepdims=True))
                    after = jnp.where(seen, after, before)
                    taken = jnp.where(seen, after, -NEGATIVE)
                weights = jnp.exp2((scores - wide(taken, tile_k // dim)) * scale)
                factor = jnp.exp2((before - after) * scale)
                top[head] = after
                acc[head] = acc[head] * wide(factor, 2) + jnp.dot(
                    weights.astype(jnp.bfloat16), v_tile, preferred_element_type=jnp.float32
                )

        @pl.when(whole == 1)
        def _():
            run(False)

        @pl.when(whole == 0)
        def _():
            run(True)

        @pl.when(work[base + 5] == 1)
        def _():
            if last:
                finish(query_index, acc)
            else:
                top_all[query_index] = top[...]
                acc_all[query_index] = acc[...]

    @pl.when(total > 0)
    def _():
        for head in range(heads):
            score_a[head] = score(0, head)

    def two(index, unused):
        handle(2 * index, score_a, score_b)

        @pl.when(2 * index + 1 < total)
        def _():
            handle(2 * index + 1, score_b, score_a)

        return 0

    lax.fori_loop(0, (total + 1) // 2, two, 0)


def attend(delta, place, lengths, counts, queries, pieces, state, last, further=0):
    rows, width = queries.shape
    piece_rows, dim = pieces[0].shape
    heads = width // dim
    tile_k = piece_rows // 2 * PAIR
    tiles = len(pieces) // PAIR
    tile_q = min(rows, BLOCK)
    steps = rows // tile_q
    first = state is None
    scalar = pl.BlockSpec(memory_space=pltpu.SMEM)
    vector = pl.BlockSpec(memory_space=pltpu.VMEM)
    top = (heads, tile_q, dim)
    acc = (heads, tile_q, 2 * dim)
    scratch = [
        pltpu.VMEM((tiles, tile_k, dim), jnp.bfloat16),
        pltpu.VMEM((tiles, tile_k, 2 * dim), jnp.bfloat16),
        pltpu.VMEM((heads, tile_q, tile_k), jnp.float32),
        pltpu.VMEM((heads, tile_q, tile_k), jnp.float32),
        pltpu.VMEM(top, jnp.float32),
        pltpu.VMEM(acc, jnp.float32),
        pltpu.VMEM((tile_q, dim), jnp.int32),
        pltpu.SMEM((counts.shape[0] + 1,), jnp.int32),
        pltpu.SMEM((FIELDS * (steps * tiles + 2),), jnp.int32),
    ]
    aliases = {}
    if last:
        out_shape = jax.ShapeDtypeStruct((rows, width), jnp.bfloat16)
        out_specs = vector
    else:
        out_shape = (
            jax.ShapeDtypeStruct((steps,) + top, jnp.float32),
            jax.ShapeDtypeStruct((steps,) + acc, jnp.float32),
        )
        out_specs = (vector, vector)
        if first:
            out_shape += (jax.ShapeDtypeStruct((1,), jnp.int32),)
            out_specs += (scalar,)
        else:
            aliases = {4 + len(pieces): 0, 5 + len(pieces): 1}
    carried = () if first else state
    pairs = steps * tiles * heads
    return pl.pallas_call(
        functools.partial(attend_kernel, (delta, tiles, heads, tile_q, first, last, further)),
        out_shape=out_shape,
        in_specs=[scalar] * 3 + [vector] * (1 + len(pieces) + len(carried)),
        out_specs=out_specs,
        scratch_shapes=scratch,
        input_output_aliases=aliases,
        compiler_params=pltpu.CompilerParams(vmem_limit_bytes=24 << 20),
        cost_estimate=pl.CostEstimate(
            flops=pairs * tile_q * tile_k * dim * 4,
            bytes_accessed=pairs * tile_q * dim * 4,
            transcendentals=pairs * tile_q * tile_k,
        ),
    )(place, lengths, counts, queries, *pieces, *carried)


def solution(mesh):
    contexts = mesh.shape["outer"] * mesh.shape["inner"]
    group = mesh.shape["head"]
    levels = contexts // PAIR
    sides = group // PAIR
    farthest = min((REACH + PAIR - 1) // PAIR, levels - 1)
    near_count = min(farthest, 2)

    def moved(value, target):
        pairs = []
        for level in range(levels):
            for member in range(PAIR):
                for side in range(sides):
                    for core in range(PAIR):
                        place = (level, member, side, core)
                        to = target(*place)
                        pairs.append(tuple(
                            ((a * PAIR + b) * sides + c) * PAIR + d for a, b, c, d in (place, to)
                        ))
        return lax.ppermute(value, AXES, pairs)

    def ahead(value, delta):
        return moved(value, lambda l, m, s, c: ((l + delta) % levels, m, s, c))

    def spread(value):
        found = []
        for across in range(PAIR):
            for along in range(sides):
                held = value
                if across or along:
                    held = moved(
                        value, lambda l, m, s, c: (l, (m + across) % PAIR, (s + along) % sides, c)
                    )
                found += [held, moved(held, lambda l, m, s, c: (l, m, s, 1 - c))]
        return found

    def layer(queries, keys, values, lengths, counts):
        device = lax.axis_index(("outer", "inner"))
        place = jnp.stack([device, lax.axis_index("head")]).astype(jnp.int32)

        def step(delta, **rest):
            return attend(
                delta, place=place, lengths=lengths, counts=counts, queries=queries, **rest
            )

        own = join(keys, values)
        near = [own] + [ahead(own, delta) for delta in range(1, near_count + 1)]
        state = None
        reach = None
        for delta in range(near_count):
            state = step(
                delta,
                pieces=spread(near[delta]),
                state=state,
                last=False,
                further=near_count + 1,
            )
            if delta == 0:
                reach = state[2]
                state = state[:2]
        delta = near_count
        pieces = spread(near[delta])
        if farthest == delta:
            return step(delta, pieces=pieces, state=state, last=True)

        def short(operands):
            _, pieces, state = operands
            return step(delta, pieces=pieces, state=state, last=True)

        def long(operands):
            near, pieces, state = operands
            state = step(delta, pieces=pieces, state=state, last=False)
            for further in range(delta + 1, farthest + 1):
                near = ahead(near, 1)
                state = step(further, pieces=spread(near), state=state, last=further == farthest)
            return state

        return lax.cond(reach[0] != 0, long, short, (near[delta], pieces, state))

    placed = (
        P(("outer", "inner"), "head"),
        P(AXES, None),
        P(AXES, None),
        P(),
        P(),
    )
    return jax.shard_map(
        layer, mesh=mesh, in_specs=placed, out_specs=P(("outer", "inner"), "head"), check_vma=False
    )
```

```python
import functools
import math

import jax
import jax.numpy as jnp
from jax import lax
from jax.experimental import pallas as pl
from jax.experimental.pallas import tpu as pltpu
from jax.sharding import PartitionSpec as P

BLOCK = 512
REACH = 7
PAIR = 2
FIELDS = 6
HEADER = 4
NEGATIVE = -1e30
AXES = ("outer", "inner", "head")


def join_kernel(keys, values, joined, semaphores):
    rows = keys.shape[0]
    copies = [
        pltpu.make_async_copy(keys, joined.at[:rows], semaphores.at[0]),
        pltpu.make_async_copy(values, joined.at[rows:], semaphores.at[1]),
    ]
    for copy in copies:
        copy.start()
    for copy in copies:
        copy.wait()


def join(keys, values):
    rows, dim = keys.shape
    return pl.pallas_call(
        join_kernel,
        out_shape=jax.ShapeDtypeStruct((2 * rows, dim), keys.dtype),
        in_specs=[pl.BlockSpec(memory_space=pltpu.MemorySpace.HBM)] * 2,
        out_specs=pl.BlockSpec(memory_space=pltpu.VMEM),
        scratch_shapes=[pltpu.SemaphoreType.DMA((2,))],
        compiler_params=pltpu.CompilerParams(vmem_limit_bytes=4 << 20),
        name="join",
    )(keys, values)


def plan_kernel(cfg, place, lengths, counts, query_source, *refs):
    groups, spread, steps, tile_q, tile_k, further = cfg
    plans = refs[: len(groups)]
    flag, queries, starts, semaphore = refs[len(groups) :]
    copy = pltpu.make_async_copy(query_source, queries, semaphore)
    copy.start()
    context = counts.shape[0]
    documents = lengths.shape[0]
    header = HEADER + documents
    device = place[0]
    head_index = place[1]
    side = head_index // PAIR

    def fill(index, total):
        starts[index] = total
        return total + counts[index] * BLOCK

    starts[context] = lax.fori_loop(0, context, fill, jnp.int32(0))
    own_start = starts[device]
    own_live = counts[device] * BLOCK

    def opening(position):
        def look(index, carry):
            edge, begin = carry
            edge = edge + lengths[index]
            return edge, jnp.where(edge <= position, edge, begin)

        return lax.fori_loop(0, documents, look, (jnp.int32(0), jnp.int32(0)))[1]

    def reaches(level, found):
        before = starts[(level - further + 1) * PAIR]
        return found | (opening(starts[level * PAIR]) < before).astype(jnp.int32)

    flag[0] = lax.fori_loop(further, context // PAIR, reaches, jnp.int32(0))

    for plan, deltas in zip(plans, groups):
        tiles = len(deltas) * PAIR * spread

        def edges(index, edge, plan=plan):
            edge = edge + lengths[index]
            plan[HEADER + index] = edge
            return edge

        lax.fori_loop(0, documents, edges, jnp.int32(0))

        def plan_queries(index, count, plan=plan, deltas=deltas, tiles=tiles):
            row = index * tile_q
            query_start = own_start + row
            query_end = query_start + tile_q - 1
            opened_low = opening(query_start)

            def plan_keys(tile, carry):
                count, opener = carry
                level = device // PAIR - (deltas[0] + tile // (PAIR * spread))
                inner = lax.rem(tile, PAIR * spread)
                member = lax.rem(device, PAIR)
                member = jnp.where(inner // spread == 1, 1 - member, member)
                source = jnp.maximum(level * PAIR + member, 0)
                offset = lax.rem(side + spread - lax.rem(inner, spread), spread) * tile_k
                key_start = starts[source] + offset
                key_end = key_start + tile_k - 1
                active = (
                    (level >= 0)
                    & (row < own_live)
                    & (offset < counts[source] * BLOCK)
                    & (key_start <= query_end)
                    & (key_end >= opened_low)
                )

                @pl.when(active)
                def _():
                    whole = (key_end <= query_start) & (key_start >= opening(key_end))
                    at = header + count * FIELDS
                    plan[at] = index
                    plan[at + 1] = tile
                    plan[at + 2] = whole.astype(jnp.int32)
                    plan[at + 3] = key_start
                    plan[at + 4] = opener
                    plan[at + 5] = 0

                return jnp.where(active, count + 1, count), jnp.where(active, 0, opener)

            after = lax.fori_loop(0, tiles, plan_keys, (count, jnp.int32(1)))[0]

            @pl.when(after > count)
            def _():
                plan[header + (after - 1) * FIELDS + 5] = 1

            return after

        total = lax.fori_loop(0, steps, plan_queries, jnp.int32(0))
        plan[header + total * FIELDS] = 0
        plan[header + total * FIELDS + 1] = 0
        plan[0] = total
        plan[1] = own_start
        plan[2] = own_live
        plan[3] = lax.rem(head_index, PAIR)

    copy.wait()


def make_plans(place, lengths, counts, queries, groups, spread, steps, tile_q, tile_k, further):
    scalar = pl.BlockSpec(memory_space=pltpu.SMEM)
    sizes = [
        HEADER + lengths.shape[0] + FIELDS * (steps * len(deltas) * PAIR * spread + 2)
        for deltas in groups
    ]
    shapes = [jax.ShapeDtypeStruct((size,), jnp.int32) for size in sizes + [1]]
    specs = [scalar] * len(shapes) + [pl.BlockSpec(memory_space=pltpu.VMEM)]
    shapes += [jax.ShapeDtypeStruct(queries.shape, queries.dtype)]
    found = pl.pallas_call(
        functools.partial(plan_kernel, (groups, spread, steps, tile_q, tile_k, further)),
        out_shape=shapes,
        in_specs=[scalar] * 3 + [pl.BlockSpec(memory_space=pltpu.MemorySpace.HBM)],
        out_specs=specs,
        scratch_shapes=[
            pltpu.SMEM((counts.shape[0] + 1,), jnp.int32),
            pltpu.SemaphoreType.DMA,
        ],
        compiler_params=pltpu.CompilerParams(vmem_limit_bytes=4 << 20),
        name="plan",
    )(place, *(in_hbm(array) for array in (lengths, counts, queries)))
    return found[:-2], found[-2], found[-1]


def in_hbm(array):
    return pltpu.with_memory_space_constraint(array, pltpu.MemorySpace.HBM)


def attend_kernel(cfg, plan, q_ref, *refs):
    tiles, heads, tile_q, first, last, documents, count = cfg
    spread = tiles // count
    piece_refs = refs[: PAIR * spread]
    refs = refs[PAIR * spread :]
    if last:
        top_all, acc_all, out_ref = refs[:3]
        refs = refs[3:]
    elif first:
        top_all, acc_all = refs[:2]
        refs = refs[2:]
    else:
        top_all, acc_all = refs[2:4]
        refs = refs[4:]
    k_all, v_all, score_a, score_b, top, acc, opened = refs
    rows = q_ref.shape[0]
    dim = k_all.shape[2]
    tile_k = k_all.shape[1]
    piece = tile_k // PAIR
    scale = math.log2(math.e) / math.sqrt(dim)
    header = HEADER + documents
    total = plan[0]
    own_start = plan[1]
    own_live = plan[2]
    core = plan[3]

    @pl.when(total > 0)
    def _():
        for tile in range(tiles):
            for step in range(PAIR):
                source = piece_refs[(tile % spread) * PAIR + step]
                base = (tile // spread) * 2 * piece
                slot = core if step == 0 else 1 - core
                at = pl.ds(pl.multiple_of(slot * piece, piece), piece)
                k_all[tile, at, :] = source[base : base + piece, :]
                v_all[tile, at, :dim] = source[base + piece : base + 2 * piece, :]
            v_all[tile, :, dim:] = jnp.ones((tile_k, dim), jnp.bfloat16)

    def finish(index, acc_ref):
        at = pl.ds(pl.multiple_of(index * tile_q, tile_q), tile_q)
        for head in range(heads):
            out_ref[at, head * dim : (head + 1) * dim] = (
                acc_ref[head, :, :dim] / acc_ref[head, :, dim:]
            ).astype(jnp.bfloat16)

    def wide(value, times):
        return jnp.concatenate([value] * times, axis=1)

    def score(item, head):
        at = pl.ds(pl.multiple_of(plan[header + item * FIELDS] * tile_q, tile_q), tile_q)
        return lax.dot_general(
            q_ref[at, head * dim : (head + 1) * dim],
            k_all[plan[header + item * FIELDS + 1]],
            (((1,), (1,)), ((), ())),
            preferred_element_type=jnp.float32,
        )

    def handle(item, current, coming):
        base = header + item * FIELDS
        query_index = plan[base]
        whole = plan[base + 2]

        @pl.when(plan[base + 4] == 1)
        def _():
            row = own_start + query_index * tile_q
            position = row + lax.broadcasted_iota(jnp.int32, (tile_q, dim), 0)

            def look(index, unused):
                edge = plan[HEADER + index]
                opened[...] = jnp.where(position >= edge, edge, opened[...])
                return unused

            opened[...] = jnp.zeros((tile_q, dim), jnp.int32)
            lax.fori_loop(0, documents, look, 0)
            if first:
                top[...] = jnp.full(top.shape, NEGATIVE, jnp.float32)
                acc[...] = jnp.zeros(acc.shape, jnp.float32)
            else:
                top[...] = top_all[query_index]
                acc[...] = acc_all[query_index]

        def run(masked):
            v_tile = v_all[plan[base + 1]]
            key_start = plan[base + 3]
            begin = opened[...]
            if masked:
                row = own_start + query_index * tile_q
                position = row + lax.broadcasted_iota(jnp.int32, (tile_q, dim), 0)
                behind = wide((position - begin).astype(jnp.uint32), tile_k // dim)
                key_position = key_start + lax.broadcasted_iota(jnp.int32, (1, tile_k), 1)
            else:
                seen = begin <= key_start
            for head in range(heads):
                coming[head] = score(item + 1, head)
                scores = current[head]
                before = top[head]
                if masked:
                    into = (key_position - wide(begin, tile_k // dim)).astype(jnp.uint32)
                    scores = jnp.where(into <= behind, scores, NEGATIVE)
                    after = jnp.maximum(before, jnp.max(scores, axis=1, keepdims=True))
                    taken = after
                else:
                    after = jnp.maximum(before, jnp.max(scores, axis=1, keepdims=True))
                    after = jnp.where(seen, after, before)
                    taken = jnp.where(seen, after, -NEGATIVE)
                weights = jnp.exp2((scores - wide(taken, tile_k // dim)) * scale)
                factor = jnp.exp2((before - after) * scale)
                top[head] = after
                acc[head] = acc[head] * wide(factor, 2) + jnp.dot(
                    weights.astype(jnp.bfloat16), v_tile, preferred_element_type=jnp.float32
                )

        @pl.when(whole == 1)
        def _():
            run(False)

        @pl.when(whole == 0)
        def _():
            run(True)

        @pl.when(plan[base + 5] == 1)
        def _():
            if last:
                finish(query_index, acc)
            else:
                top_all[query_index] = top[...]
                acc_all[query_index] = acc[...]

    @pl.when(total > 0)
    def _():
        for head in range(heads):
            score_a[head] = score(0, head)

    def two(index, unused):
        handle(2 * index, score_a, score_b)

        @pl.when(2 * index + 1 < total)
        def _():
            handle(2 * index + 1, score_b, score_a)

        return 0

    lax.fori_loop(0, (total + 1) // 2, two, 0)

    if last:

        def rest(index, following):
            row = index * tile_q
            seen = (following < total) & (plan[header + following * FIELDS] == index)

            @pl.when(jnp.logical_not(seen) & (row < own_live))
            def _():
                finish(index, acc_all.at[index])

            @pl.when(row >= own_live)
            def _():
                at = pl.ds(pl.multiple_of(row, tile_q), tile_q)
                out_ref[at, :] = jnp.zeros((tile_q, heads * dim), jnp.bfloat16)

            def skip(item, found):
                return jnp.where(plan[header + item * FIELDS] <= index, found + 1, found)

            return lax.fori_loop(0, total, skip, jnp.int32(0))

        lax.fori_loop(0, rows // tile_q, rest, jnp.int32(0))


def attend(plan, documents, count, queries, pieces, state, last):
    rows, width = queries.shape
    piece_rows, dim = pieces[0].shape
    heads = width // dim
    tile_k = piece_rows // (2 * count) * PAIR
    tiles = len(pieces) // PAIR * count
    tile_q = min(rows, BLOCK)
    steps = rows // tile_q
    first = state is None
    scalar = pl.BlockSpec(memory_space=pltpu.SMEM)
    vector = pl.BlockSpec(memory_space=pltpu.VMEM)
    top = (heads, tile_q, dim)
    acc = (heads, tile_q, 2 * dim)
    scratch = [
        pltpu.VMEM((tiles, tile_k, dim), jnp.bfloat16),
        pltpu.VMEM((tiles, tile_k, 2 * dim), jnp.bfloat16),
        pltpu.VMEM((heads, tile_q, tile_k), jnp.float32),
        pltpu.VMEM((heads, tile_q, tile_k), jnp.float32),
        pltpu.VMEM(top, jnp.float32),
        pltpu.VMEM(acc, jnp.float32),
        pltpu.VMEM((tile_q, dim), jnp.int32),
    ]
    aliases = {}
    if last:
        out_shape = jax.ShapeDtypeStruct((rows, width), jnp.bfloat16)
        out_specs = vector
    else:
        out_shape = (
            jax.ShapeDtypeStruct((steps,) + top, jnp.float32),
            jax.ShapeDtypeStruct((steps,) + acc, jnp.float32),
        )
        out_specs = (vector, vector)
        if not first:
            aliases = {2 + len(pieces): 0, 3 + len(pieces): 1}
    carried = () if first else state
    pairs = steps * tiles * heads
    return pl.pallas_call(
        functools.partial(attend_kernel, (tiles, heads, tile_q, first, last, documents, count)),
        out_shape=out_shape,
        in_specs=[scalar] + [vector] * (1 + len(pieces) + len(carried)),
        out_specs=out_specs,
        scratch_shapes=scratch,
        input_output_aliases=aliases,
        compiler_params=pltpu.CompilerParams(vmem_limit_bytes=24 << 20),
        cost_estimate=pl.CostEstimate(
            flops=pairs * tile_q * tile_k * dim * 4,
            bytes_accessed=pairs * tile_q * dim * 4,
            transcendentals=pairs * tile_q * tile_k,
        ),
    )(plan, queries, *pieces, *carried)


def solution(mesh):
    contexts = mesh.shape["outer"] * mesh.shape["inner"]
    group = mesh.shape["head"]
    levels = contexts // PAIR
    sides = group // PAIR
    farthest = min((REACH + PAIR - 1) // PAIR, levels - 1)
    near_count = min(farthest, 2)

    def moved(value, target):
        pairs = []
        for level in range(levels):
            for member in range(PAIR):
                for side in range(sides):
                    for core in range(PAIR):
                        place = (level, member, side, core)
                        to = target(*place)
                        pairs.append(tuple(
                            ((a * PAIR + b) * sides + c) * PAIR + d for a, b, c, d in (place, to)
                        ))
        return lax.ppermute(value, AXES, pairs)

    def ahead(value, delta):
        return moved(value, lambda l, m, s, c: ((l + delta) % levels, m, s, c))

    def spread(value):
        found = []
        for across in range(PAIR):
            for along in range(sides):
                held = value
                if across or along:
                    held = moved(
                        value, lambda l, m, s, c: (l, (m + across) % PAIR, (s + along) % sides, c)
                    )
                found += [held, moved(held, lambda l, m, s, c: (l, m, s, 1 - c))]
        return found

    def layer(queries, keys, values, lengths, counts):
        device = lax.axis_index(("outer", "inner"))
        place = jnp.stack([device, lax.axis_index("head")]).astype(jnp.int32)

        rows = queries.shape[0]
        tile_q = min(rows, BLOCK)
        groups = [(0,)] + [tuple(range(1, near_count + 1))] * (near_count > 0)
        groups += [(delta,) for delta in range(near_count + 1, farthest + 1)]
        plans, reach, held_queries = make_plans(
            place,
            lengths,
            counts,
            queries,
            groups,
            sides,
            rows // tile_q,
            tile_q,
            keys.shape[0] * PAIR,
            near_count + 1,
        )

        def step(index, pieces, state, last):
            return attend(
                plans[index],
                lengths.shape[0],
                len(groups[index]),
                held_queries,
                pieces,
                state,
                last,
            )

        own = join(in_hbm(keys), in_hbm(values))
        near = [ahead(own, delta) for delta in range(1, near_count + 1)]
        only = near_count == 0
        state = step(0, spread(own), None, only)
        if only:
            return state
        pieces = spread(jnp.concatenate(near, axis=0))
        if farthest == near_count:
            return step(1, pieces, state, True)

        def short(operands):
            _, pieces, state = operands
            return step(1, pieces, state, True)

        def long(operands):
            near, pieces, state = operands
            state = step(1, pieces, state, False)
            for index in range(2, len(groups)):
                near = ahead(near, 1)
                state = step(index, spread(near), state, index == len(groups) - 1)
            return state

        return lax.cond(reach[0] != 0, long, short, (near[-1], pieces, state))

    placed = (
        P(("outer", "inner"), "head"),
        P(AXES, None),
        P(AXES, None),
        P(),
        P(),
    )
    return jax.shard_map(
        layer, mesh=mesh, in_specs=placed, out_specs=P(("outer", "inner"), "head"), check_vma=False
    )
```

```python
import functools
import math

import jax
import jax.numpy as jnp
from jax import lax
from jax.experimental import pallas as pl
from jax.experimental.pallas import tpu as pltpu
from jax.sharding import PartitionSpec as P

BLOCK = 512
REACH = 7
PAIR = 2
FIELDS = 6
HEADER = 4
NEGATIVE = -1e30
AXES = ("outer", "inner", "head")


def join_kernel(keys, values, joined, semaphores):
    rows = keys.shape[0]
    copies = [
        pltpu.make_async_copy(keys, joined.at[:rows], semaphores.at[0]),
        pltpu.make_async_copy(values, joined.at[rows:], semaphores.at[1]),
    ]
    for copy in copies:
        copy.start()
    for copy in copies:
        copy.wait()


def join(keys, values):
    rows, dim = keys.shape
    return pl.pallas_call(
        join_kernel,
        out_shape=jax.ShapeDtypeStruct((2 * rows, dim), keys.dtype),
        in_specs=[pl.BlockSpec(memory_space=pltpu.MemorySpace.HBM)] * 2,
        out_specs=pl.BlockSpec(memory_space=pltpu.VMEM),
        scratch_shapes=[pltpu.SemaphoreType.DMA((2,))],
        compiler_params=pltpu.CompilerParams(vmem_limit_bytes=4 << 20),
        name="join",
    )(keys, values)


def plan_kernel(cfg, place, lengths, counts, query_source, *refs):
    groups, spread, steps, tile_q, tile_k, further = cfg
    plans = refs[: len(groups)]
    flag, queries, starts, semaphore = refs[len(groups) :]
    copy = pltpu.make_async_copy(query_source, queries, semaphore)
    copy.start()
    context = counts.shape[0]
    documents = lengths.shape[0]
    header = HEADER + documents
    device = place[0]
    head_index = place[1]
    side = head_index // PAIR

    def fill(index, total):
        starts[index] = total
        return total + counts[index] * BLOCK

    starts[context] = lax.fori_loop(0, context, fill, jnp.int32(0))
    own_start = starts[device]
    own_live = counts[device] * BLOCK

    def opening(position):
        def look(index, carry):
            edge, begin = carry
            edge = edge + lengths[index]
            return edge, jnp.where(edge <= position, edge, begin)

        return lax.fori_loop(0, documents, look, (jnp.int32(0), jnp.int32(0)))[1]

    def reaches(level, found):
        before = starts[(level - further + 1) * PAIR]
        return found | (opening(starts[level * PAIR]) < before).astype(jnp.int32)

    flag[0] = lax.fori_loop(further, context // PAIR, reaches, jnp.int32(0))

    for plan, tiles in zip(plans, groups):

        def edges(index, edge, plan=plan):
            edge = edge + lengths[index]
            plan[HEADER + index] = edge
            return edge

        lax.fori_loop(0, documents, edges, jnp.int32(0))

        def plan_queries(index, count, plan=plan, tiles=tiles):
            row = index * tile_q
            query_start = own_start + row
            query_end = query_start + tile_q - 1
            opened_low = opening(query_start)
            before = count
            for tile, (delta, across, along) in enumerate(tiles):
                level = device // PAIR - delta
                member = lax.rem(device + across, PAIR)
                source = jnp.maximum(level * PAIR + member, 0)
                offset = lax.rem(side + spread - along, spread) * tile_k
                key_start = starts[source] + offset
                key_end = key_start + tile_k - 1
                active = (
                    (level >= 0)
                    & (row < own_live)
                    & (offset < counts[source] * BLOCK)
                    & (key_start <= query_end)
                    & (key_end >= opened_low)
                )

                @pl.when(active)
                def _(count=count, tile=tile, key_start=key_start, key_end=key_end):
                    whole = (key_end <= query_start) & (key_start >= opening(key_end))
                    at = header + count * FIELDS
                    plan[at] = index
                    plan[at + 1] = tile
                    plan[at + 2] = whole.astype(jnp.int32)
                    plan[at + 3] = key_start
                    plan[at + 4] = (count == before).astype(jnp.int32)
                    plan[at + 5] = 0

                count = jnp.where(active, count + 1, count)

            @pl.when(count > before)
            def _():
                plan[header + (count - 1) * FIELDS + 5] = 1

            return count

        total = lax.fori_loop(0, steps, plan_queries, jnp.int32(0))
        plan[header + total * FIELDS] = 0
        plan[header + total * FIELDS + 1] = 0
        plan[0] = total
        plan[1] = own_start
        plan[2] = own_live
        plan[3] = lax.rem(head_index, PAIR)

    copy.wait()


def make_plans(place, lengths, counts, queries, groups, spread, steps, tile_q, tile_k, further):
    scalar = pl.BlockSpec(memory_space=pltpu.SMEM)
    sizes = [
        HEADER + lengths.shape[0] + FIELDS * (steps * len(tiles) + 2)
        for tiles in groups
    ]
    shapes = [jax.ShapeDtypeStruct((size,), jnp.int32) for size in sizes + [1]]
    specs = [scalar] * len(shapes) + [pl.BlockSpec(memory_space=pltpu.VMEM)]
    shapes += [jax.ShapeDtypeStruct(queries.shape, queries.dtype)]
    found = pl.pallas_call(
        functools.partial(plan_kernel, (groups, spread, steps, tile_q, tile_k, further)),
        out_shape=shapes,
        in_specs=[scalar] * 3 + [pl.BlockSpec(memory_space=pltpu.MemorySpace.HBM)],
        out_specs=specs,
        scratch_shapes=[
            pltpu.SMEM((counts.shape[0] + 1,), jnp.int32),
            pltpu.SemaphoreType.DMA,
        ],
        compiler_params=pltpu.CompilerParams(vmem_limit_bytes=4 << 20),
        name="plan",
    )(place, *(in_hbm(array) for array in (lengths, counts, queries)))
    return found[:-2], found[-2], found[-1]


def in_hbm(array):
    return pltpu.with_memory_space_constraint(array, pltpu.MemorySpace.HBM)


def attend_kernel(cfg, plan, q_ref, *refs):
    table, arrays, heads, tile_q, first, last, documents = cfg
    tiles = len(table)
    piece_refs = refs[:arrays]
    refs = refs[arrays:]
    if last:
        top_all, acc_all, out_hbm = refs[:3]
        out_ref, semaphores = refs[-2:]
        refs = refs[3:-2]
    elif first:
        top_all, acc_all = refs[:2]
        refs = refs[2:]
    else:
        top_all, acc_all = refs[2:4]
        refs = refs[4:]
    k_all, v_all, score_a, score_b, top, acc, opened = refs
    rows = q_ref.shape[0]
    dim = k_all.shape[2]
    tile_k = k_all.shape[1]
    piece = tile_k // PAIR
    scale = math.log2(math.e) / math.sqrt(dim)
    header = HEADER + documents
    total = plan[0]
    own_start = plan[1]
    own_live = plan[2]
    core = plan[3]

    @pl.when(total > 0)
    def _():
        for tile in range(tiles):
            for step in range(PAIR):
                source = piece_refs[table[tile][step]]
                base = table[tile][PAIR] * 2 * piece
                slot = core if step == 0 else 1 - core
                at = pl.ds(pl.multiple_of(slot * piece, piece), piece)
                k_all[tile, at, :] = source[base : base + piece, :]
                v_all[tile, at, :dim] = source[base + piece : base + 2 * piece, :]
            v_all[tile, :, dim:] = jnp.ones((tile_k, dim), jnp.bfloat16)

    def finish(index, acc_ref):
        at = pl.ds(pl.multiple_of(index * tile_q, tile_q), tile_q)
        for head in range(heads):
            out_ref[at, head * dim : (head + 1) * dim] = (
                acc_ref[head, :, :dim] / acc_ref[head, :, dim:]
            ).astype(jnp.bfloat16)
        store(index).start()

    def store(index):
        at = pl.ds(pl.multiple_of(index * tile_q, tile_q), tile_q)
        return pltpu.make_async_copy(out_ref.at[at], out_hbm.at[at], semaphores.at[index])

    def wide(value, times):
        return jnp.concatenate([value] * times, axis=1)

    def score(item, head):
        at = pl.ds(pl.multiple_of(plan[header + item * FIELDS] * tile_q, tile_q), tile_q)
        return lax.dot_general(
            q_ref[at, head * dim : (head + 1) * dim],
            k_all[plan[header + item * FIELDS + 1]],
            (((1,), (1,)), ((), ())),
            preferred_element_type=jnp.float32,
        )

    def handle(item, current, coming):
        base = header + item * FIELDS
        query_index = plan[base]
        whole = plan[base + 2]

        @pl.when(plan[base + 4] == 1)
        def _():
            row = own_start + query_index * tile_q
            position = row + lax.broadcasted_iota(jnp.int32, (tile_q, dim), 0)

            def look(index, unused):
                edge = plan[HEADER + index]
                opened[...] = jnp.where(position >= edge, edge, opened[...])
                return unused

            opened[...] = jnp.zeros((tile_q, dim), jnp.int32)
            lax.fori_loop(0, documents, look, 0)
            if first:
                top[...] = jnp.full(top.shape, NEGATIVE, jnp.float32)
                acc[...] = jnp.zeros(acc.shape, jnp.float32)
            else:
                top[...] = top_all[query_index]
                acc[...] = acc_all[query_index]

        def run(masked):
            v_tile = v_all[plan[base + 1]]
            key_start = plan[base + 3]
            begin = opened[...]
            if masked:
                row = own_start + query_index * tile_q
                position = row + lax.broadcasted_iota(jnp.int32, (tile_q, dim), 0)
                behind = wide((position - begin).astype(jnp.uint32), tile_k // dim)
                key_position = key_start + lax.broadcasted_iota(jnp.int32, (1, tile_k), 1)
            else:
                seen = begin <= key_start
            for head in range(heads):
                coming[head] = score(item + 1, head)
                scores = current[head]
                before = top[head]
                if masked:
                    into = (key_position - wide(begin, tile_k // dim)).astype(jnp.uint32)
                    scores = jnp.where(into <= behind, scores, NEGATIVE)
                    after = jnp.maximum(before, jnp.max(scores, axis=1, keepdims=True))
                    taken = after
                else:
                    after = jnp.maximum(before, jnp.max(scores, axis=1, keepdims=True))
                    after = jnp.where(seen, after, before)
                    taken = jnp.where(seen, after, -NEGATIVE)
                weights = jnp.exp2((scores - wide(taken, tile_k // dim)) * scale)
                factor = jnp.exp2((before - after) * scale)
                top[head] = after
                acc[head] = acc[head] * wide(factor, 2) + jnp.dot(
                    weights.astype(jnp.bfloat16), v_tile, preferred_element_type=jnp.float32
                )

        @pl.when(whole == 1)
        def _():
            run(False)

        @pl.when(whole == 0)
        def _():
            run(True)

        @pl.when(plan[base + 5] == 1)
        def _():
            if last:
                finish(query_index, acc)
            else:
                top_all[query_index] = top[...]
                acc_all[query_index] = acc[...]

    @pl.when(total > 0)
    def _():
        for head in range(heads):
            score_a[head] = score(0, head)

    def two(index, unused):
        handle(2 * index, score_a, score_b)

        @pl.when(2 * index + 1 < total)
        def _():
            handle(2 * index + 1, score_b, score_a)

        return 0

    lax.fori_loop(0, (total + 1) // 2, two, 0)

    if last:

        def rest(index, following):
            row = index * tile_q
            seen = (following < total) & (plan[header + following * FIELDS] == index)

            @pl.when(jnp.logical_not(seen) & (row < own_live))
            def _():
                finish(index, acc_all.at[index])

            @pl.when(row >= own_live)
            def _():
                at = pl.ds(pl.multiple_of(row, tile_q), tile_q)
                out_ref[at, :] = jnp.zeros((tile_q, heads * dim), jnp.bfloat16)
                store(index).start()

            def skip(item, found):
                return jnp.where(plan[header + item * FIELDS] <= index, found + 1, found)

            return lax.fori_loop(0, total, skip, jnp.int32(0))

        lax.fori_loop(0, rows // tile_q, rest, jnp.int32(0))
        for index in range(rows // tile_q):
            store(index).wait()


def attend(plan, documents, queries, arrays, table, piece, state, last):
    rows, width = queries.shape
    dim = arrays[0].shape[1]
    heads = width // dim
    tile_k = piece * PAIR
    tiles = len(table)
    tile_q = min(rows, BLOCK)
    steps = rows // tile_q
    first = state is None
    scalar = pl.BlockSpec(memory_space=pltpu.SMEM)
    vector = pl.BlockSpec(memory_space=pltpu.VMEM)
    top = (heads, tile_q, dim)
    acc = (heads, tile_q, 2 * dim)
    scratch = [
        pltpu.VMEM((tiles, tile_k, dim), jnp.bfloat16),
        pltpu.VMEM((tiles, tile_k, 2 * dim), jnp.bfloat16),
        pltpu.VMEM((heads, tile_q, tile_k), jnp.float32),
        pltpu.VMEM((heads, tile_q, tile_k), jnp.float32),
        pltpu.VMEM(top, jnp.float32),
        pltpu.VMEM(acc, jnp.float32),
        pltpu.VMEM((tile_q, dim), jnp.int32),
    ]
    aliases = {}
    if last:
        out_shape = pltpu.MemorySpace.HBM((rows, width), jnp.bfloat16)
        out_specs = pl.BlockSpec(memory_space=pltpu.MemorySpace.HBM)
        scratch += [
            pltpu.VMEM((rows, width), jnp.bfloat16),
            pltpu.SemaphoreType.DMA((steps,)),
        ]
    else:
        out_shape = (
            jax.ShapeDtypeStruct((steps,) + top, jnp.float32),
            jax.ShapeDtypeStruct((steps,) + acc, jnp.float32),
        )
        out_specs = (vector, vector)
        if not first:
            aliases = {2 + len(arrays): 0, 3 + len(arrays): 1}
    carried = () if first else state
    pairs = steps * tiles * heads
    return pl.pallas_call(
        functools.partial(
            attend_kernel, (table, len(arrays), heads, tile_q, first, last, documents)
        ),
        out_shape=out_shape,
        in_specs=[scalar] + [vector] * (1 + len(arrays) + len(carried)),
        out_specs=out_specs,
        scratch_shapes=scratch,
        input_output_aliases=aliases,
        compiler_params=pltpu.CompilerParams(vmem_limit_bytes=24 << 20),
        cost_estimate=pl.CostEstimate(
            flops=pairs * tile_q * tile_k * dim * 4,
            bytes_accessed=pairs * tile_q * dim * 4,
            transcendentals=pairs * tile_q * tile_k,
        ),
    )(plan, queries, *arrays, *carried)


def solution(mesh):
    contexts = mesh.shape["outer"] * mesh.shape["inner"]
    group = mesh.shape["head"]
    levels = contexts // PAIR
    sides = group // PAIR
    farthest = min((REACH + PAIR - 1) // PAIR, levels - 1)
    near_count = min(farthest, 2)

    def moved(value, target):
        pairs = []
        for level in range(levels):
            for member in range(PAIR):
                for side in range(sides):
                    for core in range(PAIR):
                        place = (level, member, side, core)
                        to = target(*place)
                        pairs.append(tuple(
                            ((a * PAIR + b) * sides + c) * PAIR + d for a, b, c, d in (place, to)
                        ))
        return lax.ppermute(value, AXES, pairs)

    def ahead(value, delta):
        return moved(value, lambda l, m, s, c: ((l + delta) % levels, m, s, c))

    def spread(value):
        found = {}
        for across in range(PAIR):
            for along in range(sides):
                held = value
                if across or along:
                    held = moved(
                        value, lambda l, m, s, c: (l, (m + across) % PAIR, (s + along) % sides, c)
                    )
                met = moved(held, lambda l, m, s, c: (l, m, s, 1 - c))
                found[across, along] = (held, met)
        return found

    def layer(queries, keys, values, lengths, counts):
        device = lax.axis_index(("outer", "inner"))
        place = jnp.stack([device, lax.axis_index("head")]).astype(jnp.int32)

        rows = queries.shape[0]
        tile_q = min(rows, BLOCK)
        ways = [(across, along) for across in range(PAIR) for along in range(sides)]
        far_range = range(1, near_count + 1)
        groups = [
            [(0, *way) for way in ways] + [(delta, *ways[0]) for delta in far_range],
            [(delta, *way) for way in ways[1:] for delta in far_range],
        ]
        groups += [
            [(delta, *way) for way in ways] for delta in range(near_count + 1, farthest + 1)
        ]
        plans, reach, held_queries = make_plans(
            place,
            lengths,
            counts,
            queries,
            groups,
            sides,
            rows // tile_q,
            tile_q,
            keys.shape[0] * PAIR,
            near_count + 1,
        )

        def step(index, held, state, last):
            arrays = []
            table = []
            for delta, across, along in groups[index]:
                stacked = 1 <= delta <= near_count
                found = held[1 if stacked else delta][across, along]
                row = []
                for value in found:
                    known = [at for at, other in enumerate(arrays) if other is value]
                    if not known:
                        arrays.append(value)
                    row.append(known[0] if known else len(arrays) - 1)
                table.append((*row, delta - 1 if stacked else 0))
            return attend(
                plans[index],
                lengths.shape[0],
                held_queries,
                arrays,
                tuple(table),
                keys.shape[0],
                state,
                last,
            )

        own = join(in_hbm(keys), in_hbm(values))
        near = [ahead(own, delta) for delta in range(1, near_count + 1)]
        held = {0: spread(own)}
        held[1] = spread(jnp.concatenate(near, axis=0))
        state = step(0, held, None, False)
        if farthest == near_count:
            return step(1, held, state, True)

        def short(operands):
            _, held, state = operands
            return step(1, held, state, True)

        def long(operands):
            near, held, state = operands
            state = step(1, held, state, False)
            for index in range(2, len(groups)):
                delta = near_count + index - 1
                near = ahead(near, 1)
                state = step(index, {delta: spread(near)}, state, index == len(groups) - 1)
            return state

        rest = {way: held[1][way] for way in ways[1:]}
        return lax.cond(reach[0] != 0, long, short, (near[-1], {1: rest}, state))

    placed = (
        P(("outer", "inner"), "head"),
        P(AXES, None),
        P(AXES, None),
        P(),
        P(),
    )
    return jax.shard_map(
        layer, mesh=mesh, in_specs=placed, out_specs=P(("outer", "inner"), "head"), check_vma=False
    )
```
